32 devices in a mesh: seq: 4 (over y, x), chan: 8 (over z, core).
Axes of the slice: x: 2, y: 2, z: 4, core: 2. Of those that a mesh axis runs over, the one named last changes fastest.
Arguments:
- query_stream: bfloat16 [2048, 8192], P('seq', 'chan'), may hold values from -6 to 6
- key_stream: bfloat16 [2048, 8192], P('seq', 'chan'), may hold values from -6 to 6
- value_stream: bfloat16 [2048, 8192], P('seq', 'chan'), may hold values from -6 to 6
- teacher_filter: float32 [512, 128], P('chan'), may hold values from -0.5 to 0.5
- student_filter: float32 [512, 128], P('chan'), may hold values from -0.5 to 0.5
- group_mask: int32 [512], P('chan'), may hold values 0 or 1
- base_ids: int32 [2048], replicated, may hold values from 0 to 7
- teacher_proj: bfloat16 [8192, 8192], P('chan', 'seq'), may hold values from -0.0625 to 0.0625
- student_proj: bfloat16 [8192, 8192], P('chan', 'seq'), may hold values from -0.09375 to 0.09375
Outputs:
- proj_grad: float32 [8192, 8192], P('chan', 'seq')
The draws below stay inside these ranges and needn't reach their ends.
All inputs are finite; a program needn't handle non-finite values. No bound on the sum of `group_mask` on one device may be relied on, other than what follows from the above.
Results may differ from the reference program's by a relative error of at most 0.022.
Values may be sent and summed in bfloat16 or wider, within the bound.
A program may use at most 128 MiB of HBM per device.

```python
import jax
import jax.numpy as jnp
from jax import lax

D = 8192
KERNEL = 128
GROUP_CH = 16
TOK_DEV = 512
TOKENS = 2048
GROUPS = 512
N_SEQ = 4
N_CHAN = 8


def with_ends(result, rng, low, largest):
    shape = result.shape
    spot = [jax.random.randint(jax.random.fold_in(rng, axis), (), 0, shape[axis]) for axis in range(len(shape))]
    result = result.at[tuple(spot)].set(low)
    longest = shape.index(max(shape))
    spot[longest] = (spot[longest] + 1) % shape[longest]
    return result.at[tuple(spot)].set(largest)


def with_spikes(entries, rng, source, target, shards_of, factor):
    def block_of(axis_at):
        return (jnp.arange(entries.shape[axis_at]) // (entries.shape[axis_at] // shards_of)).reshape((-1,) + (1,) * (entries.ndim - 1 - axis_at))

    near = jax.random.permutation(rng, shards_of)[block_of(target)]
    far = (block_of(target) + shards_of // 2) % shards_of
    return jnp.where((block_of(source) == near) | (block_of(source) == far), factor * entries, entries)


def block_levels(own_key, dims, shards, low, high):
    loudness = 1.0
    for position, shards_of in shards:
        draws = jax.random.uniform(jax.random.fold_in(jax.random.fold_in(own_key, 6), position), (shards_of,), jnp.float32, low / len(shards), high / len(shards))
        loudness = loudness * jnp.repeat(jnp.exp(draws), dims[position] // shards_of).reshape((-1,) + (1,) * (len(dims) - 1 - position))
    return loudness


def centred(rng, dims, deviation, limit, split=(), kind=jnp.bfloat16):
    drawn = jax.random.normal(rng, dims, jnp.float32) * deviation
    if len(split) > 0:
        drawn = block_levels(rng, dims, split, -0.22, 0.18) * drawn
    return jnp.clip(drawn, min=-limit, max=limit).astype(kind)


def heavy_noise(own_key, extent, deviation, bound, split, heavy, dtype=jnp.bfloat16):
    result = deviation * jax.random.normal(own_key, extent, jnp.float32)
    if split:
        result = result * block_levels(own_key, extent, split, -0.22, 0.18)
    return jnp.clip(with_spikes(result, jax.random.fold_in(own_key, 3), *heavy), -bound, bound).astype(dtype)


def setup_inputs(seed: int = 0) -> dict:
    arg_keys = jax.random.split(jax.random.key(seed), 10)
    query_stream = centred(arg_keys[0], (TOKENS, D), 1.0, 6.0, ((0, 4), (1, 8)))
    key_stream = centred(arg_keys[1], (TOKENS, D), 1.0, 6.0, ((0, 4), (1, 8)))
    value_stream = centred(arg_keys[2], (TOKENS, D), 1.0, 6.0, ((0, 4), (1, 8)))
    teacher_filter = centred(arg_keys[3], (GROUPS, KERNEL), 0.0884, 0.5, ((0, 8),), jnp.float32)
    student_filter = centred(arg_keys[4], (GROUPS, KERNEL), 0.0884, 0.5, ((0, 8),), jnp.float32)
    group_mask = with_ends((jax.random.randint(arg_keys[5], (GROUPS,), 0, 4) < 3).astype(jnp.int32), jax.random.fold_in(arg_keys[5], 1), 0, 1)
    base_ids = with_ends(jax.random.randint(arg_keys[6], (TOKENS,), 0, 8), jax.random.fold_in(arg_keys[6], 1), 0, 7).astype(jnp.int32)
    teacher_proj = centred(arg_keys[7], (D, D), D ** -0.5, 0.0625, ((0, 8), (1, 4)))
    student_proj = heavy_noise(arg_keys[8], (D, D), D ** -0.5, 0.09375, ((0, 8), (1, 4)), (0, 1, 8, 2.0))
    return dict(query_stream=query_stream, key_stream=key_stream, value_stream=value_stream, teacher_filter=teacher_filter, student_filter=student_filter, group_mask=group_mask, base_ids=base_ids, teacher_proj=teacher_proj, student_proj=student_proj)


repeat_weight = 0.1


def filter_stream(stream, filters):
    token_total = stream.shape[0]
    per_channel = jnp.repeat(filters, GROUP_CH, axis=0)
    padded = jnp.concatenate([jnp.zeros((KERNEL - 1, stream.shape[1]), jnp.float32), stream], axis=0)

    def add_tap(tap_index, accumulated):
        shifted = lax.dynamic_slice_in_dim(padded, KERNEL - 1 - tap_index, token_total, 0)
        column = lax.dynamic_slice_in_dim(per_channel, tap_index, 1, 1)[:, 0]
        return accumulated + shifted * column[None, :]

    return lax.fori_loop(0, KERNEL, add_tap, jnp.zeros(stream.shape, jnp.float32))


def reference(query_stream, key_stream, value_stream, teacher_filter, student_filter, group_mask, base_ids, teacher_proj, student_proj):
    gated = (key_stream.astype(jnp.float32) * value_stream.astype(jnp.float32)).astype(jnp.bfloat16)
    gated_wide = lax.optimization_barrier(gated).astype(jnp.float32)
    teacher_mix = filter_stream(gated_wide, teacher_filter)
    student_mix = filter_stream(gated_wide, student_filter)
    keep = jnp.repeat(group_mask.astype(jnp.float32), GROUP_CH)
    queries = query_stream.astype(jnp.float32)
    teacher_out = (queries * teacher_mix).astype(jnp.bfloat16)
    student_out = (queries * student_mix * keep[None, :]).astype(jnp.bfloat16)
    block_width = D // N_CHAN

    def add_block(block, accumulated):
        student_part = lax.dynamic_slice_in_dim(student_out, block * block_width, block_width, 1)
        teacher_part = lax.dynamic_slice_in_dim(teacher_out, block * block_width, block_width, 1)
        student_rows = lax.dynamic_slice_in_dim(student_proj, block * block_width, block_width, 0)
        teacher_rows = lax.dynamic_slice_in_dim(teacher_proj, block * block_width, block_width, 0)
        part = jnp.dot(student_part, student_rows, preferred_element_type=jnp.float32) - jnp.dot(teacher_part, teacher_rows, preferred_element_type=jnp.float32)
        return accumulated + lax.optimization_barrier(part.astype(jnp.bfloat16)).astype(jnp.float32)

    summed = lax.fori_loop(0, N_CHAN, add_block, jnp.zeros((TOKENS, D), jnp.float32))
    residual = lax.optimization_barrier(summed.astype(jnp.bfloat16)).astype(jnp.float32)
    scale = float(TOKENS) ** -0.5
    token_weight = jnp.where(base_ids >= 4, repeat_weight, 1.0).astype(jnp.float32) * scale
    adjoint = (residual * token_weight[:, None]).astype(jnp.bfloat16)

    def add_rows(block, accumulated):
        student_rows = lax.dynamic_slice_in_dim(student_out, block * TOK_DEV, TOK_DEV, 0)
        adjoint_rows = lax.dynamic_slice_in_dim(adjoint, block * TOK_DEV, TOK_DEV, 0)
        part = jnp.dot(student_rows.T, adjoint_rows, preferred_element_type=jnp.float32)
        return accumulated + lax.optimization_barrier(part.astype(jnp.bfloat16)).astype(jnp.float32)

    return lax.fori_loop(0, N_SEQ, add_rows, jnp.zeros((D, D), jnp.float32))
```

```python
import functools

import jax
import jax.numpy as jnp
from jax import lax
from jax.experimental import pallas as pl
from jax.experimental.pallas import tpu as pltpu
from jax.sharding import PartitionSpec as P

repeat_weight = 0.1
lanes = 128
halves = 2
vmem_limit = 66_000_000


def shifted(value, axis, steps):
    count = lax.axis_size(axis)
    initial, last = (max(0, -steps), min(count, count - steps))
    return lax.ppermute(value, axis, [(source, source + steps) for source in range(initial, last)])


def mix_kernel(taps, width, q_ref, k_ref, v_ref, prior_ref, rows_ref, keep_ref, out_ref, ext_ref):
    tokens = q_ref.shape[0]
    blocks = tokens // taps
    group_count = lanes // width
    gated = (k_ref[...].astype(jnp.float32) * v_ref[...].astype(jnp.float32)).astype(jnp.bfloat16)
    ext_ref[0:taps, 0:lanes] = prior_ref[...]
    for block in range(blocks):
        piece = gated[block * taps : (block + 1) * taps]
        ext_ref[taps : 2 * taps, block * lanes : (block + 1) * lanes] = piece
        if block + 1 < blocks:
            ext_ref[0:taps, (block + 1) * lanes : (block + 2) * lanes] = piece
    windows = ext_ref[...]
    lane_group = lax.broadcasted_iota(jnp.int32, (2 * taps, blocks * lanes), 1) % lanes // width
    mixed = jnp.zeros((2 * taps, blocks * lanes), jnp.float32)
    for group in range(group_count):
        tables = []
        for kind in range(2):
            base = jnp.broadcast_to(rows_ref[kind, group : group + 1, :], (taps, 2 * taps))
            tables.append(pltpu.roll(base, 0, 1, stride=1, stride_axis=0))
        table = jnp.concatenate(tables, axis=0).astype(jnp.bfloat16)
        product = jnp.dot(table, windows, preferred_element_type=jnp.float32)
        mixed = jnp.where(lane_group == group, product, mixed)
    half_rows = tokens // halves
    for block in range(blocks):
        start = block * taps
        query = q_ref[start : start + taps, :].astype(jnp.float32)
        columns = slice(block * lanes, (block + 1) * lanes)
        half, row = start // half_rows, start % half_rows
        out_ref[half, 0, row : row + taps, :] = (query * mixed[:taps, columns]).astype(jnp.bfloat16)
        out_ref[half, 1, row : row + taps, :] = (
            query * mixed[taps:, columns] * keep_ref[...]
        ).astype(jnp.bfloat16)


def flipped(position, bits):
    result = position
    step = 1
    while step <= bits:
        if bits & step:
            result = result + step - 2 * step * ((position // step) % 2)
        step *= 2
    return result


def grad_kernel(
    seq_count,
    chan_count,
    own_ref,
    teacher_hbm,
    student_hbm,
    weight_ref,
    grad_ref,
    mixes,
    teacher_w,
    student_w,
    part,
    adjoint,
    transposed,
    *rest,
):
    bits = chan_count.bit_length() - 1
    received = rest[:bits]
    local_sem, seq_send, seq_recv, down_send, down_recv, up_send, up_recv = rest[bits:]
    seq_me = lax.axis_index("seq")
    chan_me = lax.axis_index("chan")
    units = seq_count * halves
    rows = part.shape[1]
    columns = part.shape[2]
    channels = mixes.shape[3]
    tile = min(512, columns)

    local = [
        pltpu.make_async_copy(own_ref, mixes.at[pl.ds(0, halves)], local_sem.at[0]),
        pltpu.make_async_copy(teacher_hbm, teacher_w, local_sem.at[1]),
        pltpu.make_async_copy(student_hbm, student_w, local_sem.at[2]),
    ]
    for copy in local:
        copy.start()

    chan_partners = [{"seq": seq_me, "chan": flipped(chan_me, 1 << bit)} for bit in range(bits)]
    seq_partners = [{"seq": flipped(seq_me, k), "chan": chan_me} for k in range(1, seq_count)]
    barrier = pltpu.get_barrier_semaphore()
    for partner in chan_partners + seq_partners:
        pl.semaphore_signal(
            barrier, inc=1, device_id=partner, device_id_type=pl.DeviceIdType.MESH
        )
    pl.semaphore_wait(barrier, len(chan_partners) + len(seq_partners))

    def seq_copy(unit, half, partner):
        return pltpu.make_async_remote_copy(
            src_ref=mixes.at[half],
            dst_ref=mixes.at[unit],
            send_sem=seq_send.at[unit],
            recv_sem=seq_recv.at[unit],
            device_id=partner,
            device_id_type=pl.DeviceIdType.MESH,
        )

    local[0].wait()
    for k in range(1, seq_count):
        for half in range(halves):
            seq_copy(k * halves + half, half, seq_partners[k - 1]).start()
    grad_ref[...] = jnp.zeros_like(grad_ref)
    local[1].wait()
    local[2].wait()

    side = [(chan_me // (1 << bit)) % 2 for bit in range(bits)]
    held = [0]
    for bit in range(bits):
        held.append(held[bit] + side[bit] * (rows >> (bit + 1)))

    def slab(offset, size):
        return pl.ds(pl.multiple_of(offset, 16), size)

    def down_copy(bit, unit):
        size = rows >> (bit + 1)
        away = held[bit] + (1 - side[bit]) * size
        return pltpu.make_async_remote_copy(
            src_ref=part.at[unit, slab(away, size)],
            dst_ref=received[bit].at[unit],
            send_sem=down_send.at[bit, unit],
            recv_sem=down_recv.at[bit, unit],
            device_id=chan_partners[bit],
            device_id_type=pl.DeviceIdType.MESH,
        )

    def up_copy(bit, unit, incoming=False):
        size = rows >> (bit + 1)
        start = held[bit] + (1 - side[bit]) * size if incoming else held[bit + 1]
        place = adjoint.at[unit, slab(start, size)]
        return pltpu.make_async_remote_copy(
            src_ref=place,
            dst_ref=place,
            send_sem=up_send.at[bit, unit],
            recv_sem=up_recv.at[bit, unit],
            device_id=chan_partners[bit],
            device_id_type=pl.DeviceIdType.MESH,
        )

    def multiply(unit):
        @pl.when(unit >= halves)
        def _():
            seq_copy(unit, 0, seq_partners[0]).wait_recv()

        @pl.loop(0, columns // tile)
        def _(step):
            span = pl.ds(pl.multiple_of(step * tile, tile), tile)
            student = jnp.dot(
                mixes[unit, 1], student_w[:, span], preferred_element_type=jnp.float32
            )
            teacher = jnp.dot(
                mixes[unit, 0], teacher_w[:, span], preferred_element_type=jnp.float32
            )
            part[unit, :, span] = (student - teacher).astype(jnp.bfloat16)

        down_copy(0, unit).start()

    def fold(bit, unit):
        size = rows >> (bit + 1)
        down_copy(bit, unit).wait_recv()
        kept = slab(held[bit + 1], size)
        total = part[unit, kept].astype(jnp.float32) + received[bit][unit].astype(jnp.float32)
        if bit + 1 < bits:
            part[unit, kept] = total.astype(jnp.bfloat16)
            down_copy(bit + 1, unit).start()
        else:
            residual = total.astype(jnp.bfloat16).astype(jnp.float32)
            adjoint[unit, kept] = (residual * weight_ref[unit][:, 0:1]).astype(jnp.bfloat16)
            up_copy(bit, unit).start()

    def spread(bit, unit):
        up_copy(bit, unit, True).wait_recv()
        up_copy(bit - 1, unit).start()

    def accumulate(unit):
        up_copy(0, unit, True).wait_recv()
        transposed[...] = mixes[unit, 1].T

        @pl.loop(0, columns // tile)
        def _(step):
            span = pl.ds(pl.multiple_of(step * tile, tile), tile)
            grad_ref[:, span] += jnp.dot(
                transposed[...], adjoint[unit, :, span], preferred_element_type=jnp.float32
            )

    stages = [multiply]
    stages += [functools.partial(fold, bit) for bit in range(bits)]
    stages += [functools.partial(spread, bit) for bit in range(bits - 1, 0, -1)]
    stages += [accumulate]
    last = len(stages) - 1
    order = list(range(last - 1, -1, -1)) + [last]

    @pl.loop(0, units + last)
    def _(step):
        for place in order:
            unit = step - place

            @pl.when(jnp.logical_and(unit >= 0, unit < units))
            def _():
                stages[place](unit)

    for k in range(1, seq_count):
        for half in range(halves):
            seq_copy(k * halves + half, half, seq_partners[k - 1]).wait_send()

    @pl.loop(0, units)
    def _(unit):
        for bit in range(bits):
            down_copy(bit, unit).wait_send()
            up_copy(bit, unit).wait_send()


def body(
    query_stream,
    key_stream,
    value_stream,
    teacher_filter,
    student_filter,
    group_mask,
    base_ids,
    teacher_proj,
    student_proj,
):
    tok_rows, channels = query_stream.shape
    groups, taps = teacher_filter.shape
    width = channels // groups
    seq_count = lax.axis_size("seq")
    chan_count = lax.axis_size("chan")
    columns = teacher_proj.shape[1]
    scale = float(tok_rows * seq_count) ** (-0.5)

    tail = (
        key_stream[tok_rows - taps :].astype(jnp.float32)
        * value_stream[tok_rows - taps :].astype(jnp.float32)
    ).astype(jnp.bfloat16)
    prior = shifted(tail, "seq", 1)
    filters = jnp.stack([teacher_filter, student_filter])
    base_rows = jnp.concatenate(
        [
            jnp.zeros((2, groups, 1), jnp.float32),
            filters[:, :, ::-1],
            jnp.zeros((2, groups, taps - 1), jnp.float32),
        ],
        axis=2,
    )
    keep = jnp.broadcast_to(group_mask.astype(jnp.float32)[:, None], (groups, width))
    keep = keep.reshape(1, channels)
    unit_rows = tok_rows // halves
    stream_spec = pl.BlockSpec((tok_rows, lanes), lambda i: (0, i))
    mixes = pl.pallas_call(
        functools.partial(mix_kernel, taps, width),
        grid=(channels // lanes,),
        out_shape=jax.ShapeDtypeStruct((halves, 2, unit_rows, channels), jnp.bfloat16),
        in_specs=[
            stream_spec,
            stream_spec,
            stream_spec,
            pl.BlockSpec((taps, lanes), lambda i: (0, i)),
            pl.BlockSpec((2, lanes // width, 2 * taps), lambda i: (0, i, 0)),
            pl.BlockSpec((1, lanes), lambda i: (0, i)),
        ],
        out_specs=pl.BlockSpec((halves, 2, unit_rows, lanes), lambda i: (0, 0, 0, i)),
        scratch_shapes=[pltpu.VMEM((2 * taps, tok_rows // taps * lanes), jnp.bfloat16)],
        name="mix",
    )(query_stream, key_stream, value_stream, prior, base_rows, keep)

    bits = chan_count.bit_length() - 1
    units = seq_count * halves
    piece = unit_rows // chan_count
    seq_me = lax.axis_index("seq")
    chan_me = lax.axis_index("chan")
    offset = sum(((chan_me // (1 << bit)) % 2) * (unit_rows >> (bit + 1)) for bit in range(bits))
    weights = jnp.where(base_ids >= 4, repeat_weight, 1.0).astype(jnp.float32) * scale
    here = jnp.stack(
        [
            lax.dynamic_slice_in_dim(
                weights, flipped(seq_me, u // halves) * tok_rows + (u % halves) * unit_rows + offset, piece
            )
            for u in range(units)
        ]
    )
    here = jnp.broadcast_to(here[:, :, None], (units, piece, lanes))

    any_spec = pl.BlockSpec(memory_space=pl.ANY)
    vmem_spec = pl.BlockSpec(memory_space=pltpu.VMEM)
    dma = pltpu.SemaphoreType.DMA
    return pl.pallas_call(
        functools.partial(grad_kernel, seq_count, chan_count),
        out_shape=jax.ShapeDtypeStruct((channels, columns), jnp.float32),
        in_specs=[any_spec, any_spec, any_spec, vmem_spec],
        out_specs=vmem_spec,
        scratch_shapes=[
            pltpu.VMEM((units, 2, unit_rows, channels), jnp.bfloat16),
            pltpu.VMEM(teacher_proj.shape, jnp.bfloat16),
            pltpu.VMEM(student_proj.shape, jnp.bfloat16),
            pltpu.VMEM((units, unit_rows, columns), jnp.bfloat16),
            pltpu.VMEM((units, unit_rows, columns), jnp.bfloat16),
            pltpu.VMEM((channels, unit_rows), jnp.bfloat16),
            *[
                pltpu.VMEM((units, unit_rows >> (bit + 1), columns), jnp.bfloat16)
                for bit in range(bits)
            ],
            dma((3,)),
            dma((units,)),
            dma((units,)),
            dma((bits, units)),
            dma((bits, units)),
            dma((bits, units)),
            dma((bits, units)),
        ],
        compiler_params=pltpu.CompilerParams(
            collective_id=0, has_side_effects=True, vmem_limit_bytes=vmem_limit
        ),
        name="grad",
    )(mixes, teacher_proj, student_proj, here)


def solution(mesh):
    placed = (
        P("seq", "chan"),
        P("seq", "chan"),
        P("seq", "chan"),
        P("chan", None),
        P("chan", None),
        P("chan"),
        P(),
        P("chan", "seq"),
        P("chan", "seq"),
    )
    return jax.shard_map(
        body, mesh=mesh, in_specs=placed, out_specs=P("chan", "seq"), check_vma=False
    )
```

```python
import functools

import jax
import jax.numpy as jnp
from jax import lax
from jax.experimental import pallas as pl
from jax.experimental.pallas import tpu as pltpu
from jax.sharding import PartitionSpec as P

repeat_weight = 0.1
lanes = 128
halves = 2
cuts = 2
vmem_limit = 66_000_000


def shifted(value, axis, steps):
    count = lax.axis_size(axis)
    initial, last = (max(0, -steps), min(count, count - steps))
    return lax.ppermute(value, axis, [(source, source + steps) for source in range(initial, last)])


def mix_kernel(taps, width, q_ref, k_ref, v_ref, prior_ref, rows_ref, keep_ref, out_ref, ext_ref):
    tokens = q_ref.shape[0]
    blocks = tokens // taps
    group_count = lanes // width
    gated = (k_ref[...].astype(jnp.float32) * v_ref[...].astype(jnp.float32)).astype(jnp.bfloat16)
    ext_ref[0:taps, 0:lanes] = prior_ref[...]
    for block in range(blocks):
        piece = gated[block * taps : (block + 1) * taps]
        ext_ref[taps : 2 * taps, block * lanes : (block + 1) * lanes] = piece
        if block + 1 < blocks:
            ext_ref[0:taps, (block + 1) * lanes : (block + 2) * lanes] = piece
    windows = ext_ref[...]
    lane_group = lax.broadcasted_iota(jnp.int32, (2 * taps, blocks * lanes), 1) % lanes // width
    mixed = jnp.zeros((2 * taps, blocks * lanes), jnp.float32)
    for group in range(group_count):
        tables = []
        for kind in range(2):
            base = jnp.broadcast_to(rows_ref[kind, group : group + 1, :], (taps, 2 * taps))
            tables.append(pltpu.roll(base, 0, 1, stride=1, stride_axis=0))
        table = jnp.concatenate(tables, axis=0).astype(jnp.bfloat16)
        product = jnp.dot(table, windows, preferred_element_type=jnp.float32)
        mixed = jnp.where(lane_group == group, product, mixed)
    half_rows = tokens // halves
    for block in range(blocks):
        start = block * taps
        query = q_ref[start : start + taps, :].astype(jnp.float32)
        columns = slice(block * lanes, (block + 1) * lanes)
        half, row = start // half_rows, start % half_rows
        out_ref[half, 0, row : row + taps, :] = (query * mixed[:taps, columns]).astype(jnp.bfloat16)
        out_ref[half, 1, row : row + taps, :] = (
            query * mixed[taps:, columns] * keep_ref[...]
        ).astype(jnp.bfloat16)


def flipped(position, bits):
    result = position
    step = 1
    while step <= bits:
        if bits & step:
            result = result + step - 2 * step * ((position // step) % 2)
        step *= 2
    return result


def unit_order(seq_count):
    near = [k for k in (1, 2) if k < seq_count]
    order = [(0, half) for half in range(halves)]
    order += [(k, half) for half in range(halves) for k in near]
    return order + [(k, half) for k in range(3, seq_count) for half in range(halves)]


def chan_bit(position, bit):
    return (position // (1 << bit)) % 2


def middle_steps(chan_count):
    bits = chan_count.bit_length() - 1
    assert bits >= 3 and chan_count == 1 << bits
    return [(6, 2)] + [(1 << bit, bit) for bit in range(3, bits)]


def grad_kernel(
    seq_count,
    chan_count,
    own_ref,
    teacher_hbm,
    student_hbm,
    weight_ref,
    grad_ref,
    mixes,
    teacher_w,
    student_w,
    part,
    adjoint,
    transposed,
    total_ref,
    pair_in,
    edge_in,
    *rest,
):
    steps = middle_steps(chan_count)
    count = len(steps)
    middle_in = rest[:count]
    (
        local_sem,
        seq_send,
        seq_recv,
        pair_send,
        pair_recv,
        edge_send,
        edge_recv,
        down_send,
        down_recv,
        up_send,
        up_recv,
    ) = rest[count:]
    seq_me = lax.axis_index("seq")
    chan_me = lax.axis_index("chan")
    order = unit_order(seq_count)
    items = len(order) * cuts
    rows = part.shape[1]
    columns = part.shape[2]
    tile = min(512, columns)

    local = [
        pltpu.make_async_copy(own_ref, mixes.at[pl.ds(0, halves)], local_sem.at[0]),
        pltpu.make_async_copy(teacher_hbm, teacher_w, local_sem.at[1]),
        pltpu.make_async_copy(student_hbm, student_w, local_sem.at[2]),
    ]
    for copy in local:
        copy.start()

    def along_chan(flips):
        return {"seq": seq_me, "chan": flipped(chan_me, flips)}

    pair_partner = along_chan(1)
    edge_partner = along_chan(2)
    middle_partners = [along_chan(flips) for flips, _ in steps]
    seq_partners = [{"seq": flipped(seq_me, k), "chan": chan_me} for k in range(1, seq_count)]
    everyone = [pair_partner, edge_partner] + middle_partners + seq_partners
    barrier = pltpu.get_barrier_semaphore()
    for partner in everyone:
        pl.semaphore_signal(
            barrier, inc=1, device_id=partner, device_id_type=pl.DeviceIdType.MESH
        )
    pl.semaphore_wait(barrier, len(everyone))

    def remote(source, target, send_sem, recv_sem, partner):
        return pltpu.make_async_remote_copy(
            src_ref=source,
            dst_ref=target,
            send_sem=send_sem,
            recv_sem=recv_sem,
            device_id=partner,
            device_id_type=pl.DeviceIdType.MESH,
        )

    def seq_copy(unit, half, partner):
        return remote(
            mixes.at[half], mixes.at[unit], seq_send.at[unit], seq_recv.at[unit], partner
        )

    local[0].wait()
    for unit in range(halves, len(order)):
        k, half = order[unit]
        seq_copy(unit, half, seq_partners[k - 1]).start()
    total_ref[...] = jnp.zeros_like(total_ref)
    local[1].wait()
    local[2].wait()

    half_size = rows // 2
    core = chan_bit(chan_me, 0)
    inner = chan_bit(chan_me, 1) != chan_bit(chan_me, 2)
    mine = core * half_size
    others = (1 - core) * half_size
    held = [mine]
    away = []
    for index, (_, bit) in enumerate(steps):
        size = half_size >> (index + 1)
        side = chan_bit(chan_me, bit)
        away.append(held[index] + (1 - side) * size)
        held.append(held[index] + side * size)

    def slab(offset, size):
        return pl.ds(pl.multiple_of(offset, 16), size)

    def pair_down(item):
        source = part.at[item, slab(others, half_size)]
        return remote(
            source, pair_in.at[item], pair_send.at[0, item], pair_recv.at[0, item], pair_partner
        )

    def pair_up(item, incoming=False):
        place = adjoint.at[item, slab(others if incoming else mine, half_size)]
        return remote(place, place, pair_send.at[1, item], pair_recv.at[1, item], pair_partner)

    def edge_down(item):
        source = part.at[item, slab(mine, half_size)]
        return remote(
            source, edge_in.at[item], edge_send.at[0, item], edge_recv.at[0, item], edge_partner
        )

    def edge_up(item):
        place = adjoint.at[item, slab(mine, half_size)]
        return remote(place, place, edge_send.at[1, item], edge_recv.at[1, item], edge_partner)

    def middle_down(index, item):
        source = part.at[item, slab(away[index], half_size >> (index + 1))]
        return remote(
            source,
            middle_in[index].at[item],
            down_send.at[index, item],
            down_recv.at[index, item],
            middle_partners[index],
        )

    def middle_up(index, item, incoming=False):
        start = away[index] if incoming else held[index + 1]
        place = adjoint.at[item, slab(start, half_size >> (index + 1))]
        return remote(
            place,
            place,
            up_send.at[index, item],
            up_recv.at[index, item],
            middle_partners[index],
        )

    def multiply(item):
        unit = item // cuts
        first = item % cuts * columns

        @pl.when(jnp.logical_and(unit >= halves, item % cuts == 0))
        def _():
            seq_copy(unit, 0, seq_partners[0]).wait_recv()

        @pl.loop(0, columns // tile)
        def _(step):
            span = pl.ds(pl.multiple_of(step * tile, tile), tile)
            source = pl.ds(pl.multiple_of(first + step * tile, tile), tile)
            student = jnp.dot(
                mixes[unit, 1], student_w[:, source], preferred_element_type=jnp.float32
            )
            teacher = jnp.dot(
                mixes[unit, 0], teacher_w[:, source], preferred_element_type=jnp.float32
            )
            part[item, :, span] = (student - teacher).astype(jnp.bfloat16)

        pair_down(item).start()

    def added(item, offset, size, arrived):
        kept = part[item, slab(offset, size)].astype(jnp.float32)
        return kept + arrived[item].astype(jnp.float32)

    def fold_pair(item):
        pair_down(item).wait_recv()
        part[item, slab(mine, half_size)] = added(item, mine, half_size, pair_in).astype(
            jnp.bfloat16
        )

        @pl.when(jnp.logical_not(inner))
        def _():
            edge_down(item).start()

    def fold_edge(item):
        @pl.when(inner)
        def _():
            edge_down(item).wait_recv()
            part[item, slab(mine, half_size)] = added(item, mine, half_size, edge_in).astype(
                jnp.bfloat16
            )
            middle_down(0, item).start()

    def fold_middle(index, item):
        @pl.when(inner)
        def _():
            middle_down(index, item).wait_recv()
            size = half_size >> (index + 1)
            start = held[index + 1]
            total = added(item, start, size, middle_in[index])
            if index + 1 < count:
                part[item, slab(start, size)] = total.astype(jnp.bfloat16)
                middle_down(index + 1, item).start()
            else:
                residual = total.astype(jnp.bfloat16).astype(jnp.float32)
                adjoint[item, slab(start, size)] = (
                    residual * weight_ref[item // cuts][:, 0:1]
                ).astype(jnp.bfloat16)
                middle_up(index, item).start()

    def spread_middle(index, item):
        @pl.when(inner)
        def _():
            middle_up(index, item, True).wait_recv()
            if index > 0:
                middle_up(index - 1, item).start()
            else:
                edge_up(item).start()
                pair_up(item).start()

    def spread_edge(item):
        @pl.when(jnp.logical_not(inner))
        def _():
            edge_up(item).wait_recv()
            pair_up(item).start()

    def accumulate(item):
        unit = item // cuts
        first = item % cuts * columns
        pair_up(item, True).wait_recv()

        @pl.when(item % cuts == 0)
        def _():
            transposed[...] = mixes[unit, 1].T

        @pl.loop(0, columns // tile)
        def _(step):
            span = pl.ds(pl.multiple_of(step * tile, tile), tile)
            target = pl.ds(pl.multiple_of(first + step * tile, tile), tile)
            total_ref[:, target] += jnp.dot(
                transposed[...], adjoint[item, :, span], preferred_element_type=jnp.float32
            )

    stages = [multiply, fold_pair, fold_edge]
    stages += [functools.partial(fold_middle, index) for index in range(count)]
    stages += [functools.partial(spread_middle, index) for index in range(count - 1, -1, -1)]
    stages += [spread_edge, accumulate]
    last = len(stages) - 1
    places = list(range(last - 1, -1, -1)) + [last]

    @pl.loop(0, items + last)
    def _(step):
        for place in places:
            item = step - place

            @pl.when(jnp.logical_and(item >= 0, item < items))
            def _():
                stages[place](item)

    grad_ref[...] = total_ref[...].astype(grad_ref.dtype)

    for unit in range(halves, len(order)):
        k, half = order[unit]
        seq_copy(unit, half, seq_partners[k - 1]).wait_send()

    @pl.loop(0, items)
    def _(item):
        pair_down(item).wait_send()
        pair_up(item).wait_send()

        @pl.when(inner)
        def _():
            edge_up(item).wait_send()
            for index in range(count):
                middle_down(index, item).wait_send()
                middle_up(index, item).wait_send()

        @pl.when(jnp.logical_not(inner))
        def _():
            edge_down(item).wait_send()


def body(
    query_stream,
    key_stream,
    value_stream,
    teacher_filter,
    student_filter,
    group_mask,
    base_ids,
    teacher_proj,
    student_proj,
):
    tok_rows, channels = query_stream.shape
    groups, taps = teacher_filter.shape
    width = channels // groups
    seq_count = lax.axis_size("seq")
    chan_count = lax.axis_size("chan")
    columns = teacher_proj.shape[1]
    scale = float(tok_rows * seq_count) ** (-0.5)

    tail = (
        key_stream[tok_rows - taps :].astype(jnp.float32)
        * value_stream[tok_rows - taps :].astype(jnp.float32)
    ).astype(jnp.bfloat16)
    prior = shifted(tail, "seq", 1)
    filters = jnp.stack([teacher_filter, student_filter])
    base_rows = jnp.concatenate(
        [
            jnp.zeros((2, groups, 1), jnp.float32),
            filters[:, :, ::-1],
            jnp.zeros((2, groups, taps - 1), jnp.float32),
        ],
        axis=2,
    )
    keep = jnp.broadcast_to(group_mask.astype(jnp.float32)[:, None], (groups, width))
    keep = keep.reshape(1, channels)
    unit_rows = tok_rows // halves
    stream_spec = pl.BlockSpec((tok_rows, lanes), lambda i: (0, i))
    mixes = pl.pallas_call(
        functools.partial(mix_kernel, taps, width),
        grid=(channels // lanes,),
        out_shape=jax.ShapeDtypeStruct((halves, 2, unit_rows, channels), jnp.bfloat16),
        in_specs=[
            stream_spec,
            stream_spec,
            stream_spec,
            pl.BlockSpec((taps, lanes), lambda i: (0, i)),
            pl.BlockSpec((2, lanes // width, 2 * taps), lambda i: (0, i, 0)),
            pl.BlockSpec((1, lanes), lambda i: (0, i)),
        ],
        out_specs=pl.BlockSpec((halves, 2, unit_rows, lanes), lambda i: (0, 0, 0, i)),
        scratch_shapes=[pltpu.VMEM((2 * taps, tok_rows // taps * lanes), jnp.bfloat16)],
        name="mix",
    )(query_stream, key_stream, value_stream, prior, base_rows, keep)

    order = unit_order(seq_count)
    units = len(order)
    items = units * cuts
    steps = middle_steps(chan_count)
    half_size = unit_rows // 2
    piece = half_size >> len(steps)
    seq_me = lax.axis_index("seq")
    chan_me = lax.axis_index("chan")
    offset = chan_bit(chan_me, 0) * half_size + sum(
        chan_bit(chan_me, bit) * (half_size >> (index + 1)) for index, (_, bit) in enumerate(steps)
    )
    weights = jnp.where(base_ids >= 4, repeat_weight, 1.0).astype(jnp.float32) * scale
    here = jnp.stack(
        [
            lax.dynamic_slice_in_dim(
                weights, flipped(seq_me, k) * tok_rows + half * unit_rows + offset, piece
            )
            for k, half in order
        ]
    )
    here = jnp.broadcast_to(here[:, :, None], (units, piece, lanes))

    any_spec = pl.BlockSpec(memory_space=pl.ANY)
    vmem_spec = pl.BlockSpec(memory_space=pltpu.VMEM)
    dma = pltpu.SemaphoreType.DMA
    cut = columns // cuts
    result = pl.pallas_call(
        functools.partial(grad_kernel, seq_count, chan_count),
        out_shape=jax.ShapeDtypeStruct((channels, columns), jnp.bfloat16),
        in_specs=[any_spec, any_spec, any_spec, vmem_spec],
        out_specs=vmem_spec,
        scratch_shapes=[
            pltpu.VMEM((units, 2, unit_rows, channels), jnp.bfloat16),
            pltpu.VMEM(teacher_proj.shape, jnp.bfloat16),
            pltpu.VMEM(student_proj.shape, jnp.bfloat16),
            pltpu.VMEM((items, unit_rows, cut), jnp.bfloat16),
            pltpu.VMEM((items, unit_rows, cut), jnp.bfloat16),
            pltpu.VMEM((channels, unit_rows), jnp.bfloat16),
            pltpu.VMEM((channels, columns), jnp.float32),
            pltpu.VMEM((items, half_size, cut), jnp.bfloat16),
            pltpu.VMEM((items, half_size, cut), jnp.bfloat16),
            *[
                pltpu.VMEM((items, half_size >> (index + 1), cut), jnp.bfloat16)
                for index in range(len(steps))
            ],
            dma((3,)),
            dma((units,)),
            dma((units,)),
            dma((2, items)),
            dma((2, items)),
            dma((2, items)),
            dma((2, items)),
            dma((len(steps), items)),
            dma((len(steps), items)),
            dma((len(steps), items)),
            dma((len(steps), items)),
        ],
        compiler_params=pltpu.CompilerParams(
            collective_id=0, has_side_effects=True, vmem_limit_bytes=vmem_limit
        ),
        name="grad",
    )(mixes, teacher_proj, student_proj, here)
    return result.astype(jnp.float32)


def solution(mesh):
    placed = (
        P("seq", "chan"),
        P("seq", "chan"),
        P("seq", "chan"),
        P("chan", None),
        P("chan", None),
        P("chan"),
        P(),
        P("chan", "seq"),
        P("chan", "seq"),
    )
    return jax.shard_map(
        body, mesh=mesh, in_specs=placed, out_specs=P("chan", "seq"), check_vma=False
    )
```

```python
import functools

import jax
import jax.numpy as jnp
from jax import lax
from jax.experimental import pallas as pl
from jax.experimental.pallas import tpu as pltpu
from jax.sharding import PartitionSpec as P

repeat_weight = 0.1
lanes = 128
halves = 2
cuts = 4
lag = 2
vmem_limit = 66_000_000


def shifted(value, axis, steps):
    count = lax.axis_size(axis)
    initial, last = (max(0, -steps), min(count, count - steps))
    return lax.ppermute(value, axis, [(source, source + steps) for source in range(initial, last)])


def mix_kernel(taps, width, q_ref, k_ref, v_ref, prior_ref, rows_ref, keep_ref, out_ref, ext_ref):
    tokens = q_ref.shape[0]
    blocks = tokens // taps
    group_count = lanes // width
    gated = (k_ref[...].astype(jnp.float32) * v_ref[...].astype(jnp.float32)).astype(jnp.bfloat16)
    ext_ref[0:taps, 0:lanes] = prior_ref[...]
    for block in range(blocks):
        piece = gated[block * taps : (block + 1) * taps]
        ext_ref[taps : 2 * taps, block * lanes : (block + 1) * lanes] = piece
        if block + 1 < blocks:
            ext_ref[0:taps, (block + 1) * lanes : (block + 2) * lanes] = piece
    windows = ext_ref[...]
    lane_group = lax.broadcasted_iota(jnp.int32, (2 * taps, blocks * lanes), 1) % lanes // width
    mixed = jnp.zeros((2 * taps, blocks * lanes), jnp.float32)
    for group in range(group_count):
        tables = []
        for kind in range(2):
            base = jnp.broadcast_to(rows_ref[kind, group : group + 1, :], (taps, 2 * taps))
            tables.append(pltpu.roll(base, 0, 1, stride=1, stride_axis=0))
        table = jnp.concatenate(tables, axis=0).astype(jnp.bfloat16)
        product = jnp.dot(table, windows, preferred_element_type=jnp.float32)
        mixed = jnp.where(lane_group == group, product, mixed)
    half_rows = tokens // halves
    for block in range(blocks):
        start = block * taps
        query = q_ref[start : start + taps, :].astype(jnp.float32)
        columns = slice(block * lanes, (block + 1) * lanes)
        half, row = start // half_rows, start % half_rows
        out_ref[half, 0, row : row + taps, :] = (query * mixed[:taps, columns]).astype(jnp.bfloat16)
        out_ref[half, 1, row : row + taps, :] = (
            query * mixed[taps:, columns] * keep_ref[...]
        ).astype(jnp.bfloat16)


def flipped(position, bits):
    result = position
    step = 1
    while step <= bits:
        if bits & step:
            result = result + step - 2 * step * ((position // step) % 2)
        step *= 2
    return result


def unit_order(seq_count):
    assert seq_count >= 4
    order = [(0, half) for half in range(halves)] + [(1, 0), (2, 1), (1, 1), (2, 0)]
    return order + [(k, half) for k in range(3, seq_count) for half in range(halves)]


def chan_bit(position, bit):
    return (position // (1 << bit)) % 2


def middle_steps(chan_count):
    bits = chan_count.bit_length() - 1
    assert bits >= 3 and chan_count == 1 << bits
    return [(6, 2)] + [(1 << bit, bit) for bit in range(3, bits)]


def grad_kernel(
    seq_count,
    chan_count,
    own_ref,
    teacher_hbm,
    student_hbm,
    weight_ref,
    grad_ref,
    mixes,
    teacher_w,
    student_w,
    part,
    adjoint,
    transposed,
    total_ref,
    pair_in,
    edge_in,
    *rest,
):
    steps = middle_steps(chan_count)
    count = len(steps)
    middle_in = rest[:count]
    (
        local_sem,
        seq_send,
        seq_recv,
        pair_send,
        pair_recv,
        edge_send,
        edge_recv,
        down_send,
        down_recv,
        up_send,
        up_recv,
    ) = rest[count:]
    seq_me = lax.axis_index("seq")
    chan_me = lax.axis_index("chan")
    order = unit_order(seq_count)
    items = len(order) * cuts
    rows = part.shape[1]
    columns = part.shape[2]
    tile = min(512, columns)

    local = [
        pltpu.make_async_copy(own_ref, mixes.at[pl.ds(0, halves)], local_sem.at[0]),
        pltpu.make_async_copy(teacher_hbm, teacher_w, local_sem.at[1]),
        pltpu.make_async_copy(student_hbm, student_w, local_sem.at[2]),
    ]
    for copy in local:
        copy.start()

    def along_chan(flips):
        return {"seq": seq_me, "chan": flipped(chan_me, flips)}

    pair_partner = along_chan(1)
    edge_partner = along_chan(2)
    middle_partners = [along_chan(flips) for flips, _ in steps]
    seq_partners = [{"seq": flipped(seq_me, k), "chan": chan_me} for k in range(1, seq_count)]
    everyone = [pair_partner, edge_partner] + middle_partners + seq_partners
    barrier = pltpu.get_barrier_semaphore()
    for partner in everyone:
        pl.semaphore_signal(
            barrier, inc=1, device_id=partner, device_id_type=pl.DeviceIdType.MESH
        )
    pl.semaphore_wait(barrier, len(everyone))

    def remote(source, target, send_sem, recv_sem, partner):
        return pltpu.make_async_remote_copy(
            src_ref=source,
            dst_ref=target,
            send_sem=send_sem,
            recv_sem=recv_sem,
            device_id=partner,
            device_id_type=pl.DeviceIdType.MESH,
        )

    def seq_copy(unit, half, partner):
        return remote(
            mixes.at[half], mixes.at[unit], seq_send.at[unit], seq_recv.at[unit], partner
        )

    local[0].wait()
    for unit in range(halves, len(order)):
        k, half = order[unit]
        if k != 3:
            seq_copy(unit, half, seq_partners[k - 1]).start()
    total_ref[...] = jnp.zeros_like(total_ref)
    local[1].wait()
    local[2].wait()

    half_size = rows // 2
    core = chan_bit(chan_me, 0)
    inner = chan_bit(chan_me, 1) != chan_bit(chan_me, 2)
    mine = core * half_size
    others = (1 - core) * half_size
    held = [mine]
    away = []
    for index, (_, bit) in enumerate(steps):
        size = half_size >> (index + 1)
        side = chan_bit(chan_me, bit)
        away.append(held[index] + (1 - side) * size)
        held.append(held[index] + side * size)

    def slab(offset, size):
        return pl.ds(pl.multiple_of(offset, 16), size)

    def pair_down(item):
        source = part.at[item, slab(others, half_size)]
        return remote(
            source, pair_in.at[item], pair_send.at[0, item], pair_recv.at[0, item], pair_partner
        )

    def pair_up(item, incoming=False):
        place = adjoint.at[item, slab(others if incoming else mine, half_size)]
        return remote(place, place, pair_send.at[1, item], pair_recv.at[1, item], pair_partner)

    def edge_down(item):
        source = part.at[item, slab(mine, half_size)]
        return remote(
            source, edge_in.at[item], edge_send.at[0, item], edge_recv.at[0, item], edge_partner
        )

    def edge_up(item):
        place = adjoint.at[item, slab(mine, half_size)]
        return remote(place, place, edge_send.at[1, item], edge_recv.at[1, item], edge_partner)

    def middle_down(index, item):
        source = part.at[item, slab(away[index], half_size >> (index + 1))]
        return remote(
            source,
            middle_in[index].at[item],
            down_send.at[index, item],
            down_recv.at[index, item],
            middle_partners[index],
        )

    def middle_up(index, item, incoming=False):
        start = away[index] if incoming else held[index + 1]
        place = adjoint.at[item, slab(start, half_size >> (index + 1))]
        return remote(
            place,
            place,
            up_send.at[index, item],
            up_recv.at[index, item],
            middle_partners[index],
        )

    def multiply(item):
        unit = item // cuts
        first = item % cuts * columns

        @pl.when(jnp.logical_and(unit >= halves, item % cuts == 0))
        def _():
            seq_copy(unit, 0, seq_partners[0]).wait_recv()

        for near, half in ((1, 0), (2, 1)):
            slot = order.index((near, half))
            far = order.index((3, half))

            @pl.when(item == slot * cuts)
            def _():
                remote(
                    mixes.at[slot],
                    mixes.at[far],
                    seq_send.at[far],
                    seq_recv.at[far],
                    seq_partners[2 - near],
                ).start()

        @pl.loop(0, columns // tile)
        def _(step):
            span = pl.ds(pl.multiple_of(step * tile, tile), tile)
            source = pl.ds(pl.multiple_of(first + step * tile, tile), tile)
            student = jnp.dot(
                mixes[unit, 1], student_w[:, source], preferred_element_type=jnp.float32
            )
            teacher = jnp.dot(
                mixes[unit, 0], teacher_w[:, source], preferred_element_type=jnp.float32
            )
            part[item, :, span] = (student - teacher).astype(jnp.bfloat16)

        pair_down(item).start()

    def added(item, offset, size, arrived):
        kept = part[item, slab(offset, size)].astype(jnp.float32)
        return kept + arrived[item].astype(jnp.float32)

    def fold_pair(item):
        pair_down(item).wait_recv()
        part[item, slab(mine, half_size)] = added(item, mine, half_size, pair_in).astype(
            jnp.bfloat16
        )

        @pl.when(jnp.logical_not(inner))
        def _():
            edge_down(item).start()

    def fold_edge(item):
        @pl.when(inner)
        def _():
            edge_down(item).wait_recv()
            part[item, slab(mine, half_size)] = added(item, mine, half_size, edge_in).astype(
                jnp.bfloat16
            )
            middle_down(0, item).start()

    def fold_middle(index, item):
        @pl.when(inner)
        def _():
            middle_down(index, item).wait_recv()
            size = half_size >> (index + 1)
            start = held[index + 1]
            total = added(item, start, size, middle_in[index])
            if index + 1 < count:
                part[item, slab(start, size)] = total.astype(jnp.bfloat16)
                middle_down(index + 1, item).start()
            else:
                residual = total.astype(jnp.bfloat16).astype(jnp.float32)
                adjoint[item, slab(start, size)] = (
                    residual * weight_ref[item // cuts][:, 0:1]
                ).astype(jnp.bfloat16)
                middle_up(index, item).start()

    def spread_middle(index, item):
        @pl.when(inner)
        def _():
            middle_up(index, item, True).wait_recv()
            if index > 0:
                middle_up(index - 1, item).start()
            else:
                edge_up(item).start()
                pair_up(item).start()

    def spread_edge(item):
        @pl.when(jnp.logical_not(inner))
        def _():
            edge_up(item).wait_recv()
            pair_up(item).start()

    def accumulate(item):
        unit = item // cuts
        first = item % cuts * columns
        pair_up(item, True).wait_recv()

        @pl.when(item % cuts == 0)
        def _():
            transposed[...] = mixes[unit, 1].T

        @pl.loop(0, columns // tile)
        def _(step):
            span = pl.ds(pl.multiple_of(step * tile, tile), tile)
            target = pl.ds(pl.multiple_of(first + step * tile, tile), tile)
            total_ref[:, target] += jnp.dot(
                transposed[...], adjoint[item, :, span], preferred_element_type=jnp.float32
            )

    stages = [multiply, fold_pair, fold_edge]
    stages += [functools.partial(fold_middle, index) for index in range(count)]
    stages += [functools.partial(spread_middle, index) for index in range(count - 1, -1, -1)]
    stages += [spread_edge, accumulate]
    last = len(stages) - 1
    places = list(range(last - 1, -1, -1)) + [last]

    @pl.loop(0, items + lag * last)
    def _(step):
        for place in places:
            item = step - lag * place

            @pl.when(jnp.logical_and(item >= 0, item < items))
            def _():
                stages[place](item)

    grad_ref[...] = total_ref[...].astype(grad_ref.dtype)

    for unit in range(halves, len(order)):
        k, half = order[unit]
        seq_copy(unit, half, seq_partners[k - 1]).wait_send()

    @pl.loop(0, items)
    def _(item):
        pair_down(item).wait_send()
        pair_up(item).wait_send()

        @pl.when(inner)
        def _():
            edge_up(item).wait_send()
            for index in range(count):
                middle_down(index, item).wait_send()
                middle_up(index, item).wait_send()

        @pl.when(jnp.logical_not(inner))
        def _():
            edge_down(item).wait_send()


def body(
    query_stream,
    key_stream,
    value_stream,
    teacher_filter,
    student_filter,
    group_mask,
    base_ids,
    teacher_proj,
    student_proj,
):
    tok_rows, channels = query_stream.shape
    groups, taps = teacher_filter.shape
    width = channels // groups
    seq_count = lax.axis_size("seq")
    chan_count = lax.axis_size("chan")
    columns = teacher_proj.shape[1]
    scale = float(tok_rows * seq_count) ** (-0.5)

    tail = (
        key_stream[tok_rows - taps :].astype(jnp.float32)
        * value_stream[tok_rows - taps :].astype(jnp.float32)
    ).astype(jnp.bfloat16)
    prior = shifted(tail, "seq", 1)
    filters = jnp.stack([teacher_filter, student_filter])
    base_rows = jnp.concatenate(
        [
            jnp.zeros((2, groups, 1), jnp.float32),
            filters[:, :, ::-1],
            jnp.zeros((2, groups, taps - 1), jnp.float32),
        ],
        axis=2,
    )
    keep = jnp.broadcast_to(group_mask.astype(jnp.float32)[:, None], (groups, width))
    keep = keep.reshape(1, channels)
    unit_rows = tok_rows // halves
    stream_spec = pl.BlockSpec((tok_rows, lanes), lambda i: (0, i))
    mixes = pl.pallas_call(
        functools.partial(mix_kernel, taps, width),
        grid=(channels // lanes,),
        out_shape=jax.ShapeDtypeStruct((halves, 2, unit_rows, channels), jnp.bfloat16),
        in_specs=[
            stream_spec,
            stream_spec,
            stream_spec,
            pl.BlockSpec((taps, lanes), lambda i: (0, i)),
            pl.BlockSpec((2, lanes // width, 2 * taps), lambda i: (0, i, 0)),
            pl.BlockSpec((1, lanes), lambda i: (0, i)),
        ],
        out_specs=pl.BlockSpec((halves, 2, unit_rows, lanes), lambda i: (0, 0, 0, i)),
        scratch_shapes=[pltpu.VMEM((2 * taps, tok_rows // taps * lanes), jnp.bfloat16)],
        name="mix",
    )(query_stream, key_stream, value_stream, prior, base_rows, keep)

    order = unit_order(seq_count)
    units = len(order)
    items = units * cuts
    steps = middle_steps(chan_count)
    half_size = unit_rows // 2
    piece = half_size >> len(steps)
    seq_me = lax.axis_index("seq")
    chan_me = lax.axis_index("chan")
    offset = chan_bit(chan_me, 0) * half_size + sum(
        chan_bit(chan_me, bit) * (half_size >> (index + 1)) for index, (_, bit) in enumerate(steps)
    )
    weights = jnp.where(base_ids >= 4, repeat_weight, 1.0).astype(jnp.float32) * scale
    here = jnp.stack(
        [
            lax.dynamic_slice_in_dim(
                weights, flipped(seq_me, k) * tok_rows + half * unit_rows + offset, piece
            )
            for k, half in order
        ]
    )
    here = jnp.broadcast_to(here[:, :, None], (units, piece, lanes))

    any_spec = pl.BlockSpec(memory_space=pl.ANY)
    vmem_spec = pl.BlockSpec(memory_space=pltpu.VMEM)
    dma = pltpu.SemaphoreType.DMA
    cut = columns // cuts
    result = pl.pallas_call(
        functools.partial(grad_kernel, seq_count, chan_count),
        out_shape=jax.ShapeDtypeStruct((channels, columns), jnp.bfloat16),
        in_specs=[any_spec, any_spec, any_spec, vmem_spec],
        out_specs=vmem_spec,
        scratch_shapes=[
            pltpu.VMEM((units, 2, unit_rows, channels), jnp.bfloat16),
            pltpu.VMEM(teacher_proj.shape, jnp.bfloat16),
            pltpu.VMEM(student_proj.shape, jnp.bfloat16),
            pltpu.VMEM((items, unit_rows, cut), jnp.bfloat16),
            pltpu.VMEM((items, unit_rows, cut), jnp.bfloat16),
            pltpu.VMEM((channels, unit_rows), jnp.bfloat16),
            pltpu.VMEM((channels, columns), jnp.float32),
            pltpu.VMEM((items, half_size, cut), jnp.bfloat16),
            pltpu.VMEM((items, half_size, cut), jnp.bfloat16),
            *[
                pltpu.VMEM((items, half_size >> (index + 1), cut), jnp.bfloat16)
                for index in range(len(steps))
            ],
            dma((3,)),
            dma((units,)),
            dma((units,)),
            dma((2, items)),
            dma((2, items)),
            dma((2, items)),
            dma((2, items)),
            dma((len(steps), items)),
            dma((len(steps), items)),
            dma((len(steps), items)),
            dma((len(steps), items)),
        ],
        compiler_params=pltpu.CompilerParams(
            collective_id=0, has_side_effects=True, vmem_limit_bytes=vmem_limit
        ),
        name="grad",
    )(mixes, teacher_proj, student_proj, here)
    return result.astype(jnp.float32)


def solution(mesh):
    placed = (
        P("seq", "chan"),
        P("seq", "chan"),
        P("seq", "chan"),
        P("chan", None),
        P("chan", None),
        P("chan"),
        P(),
        P("chan", "seq"),
        P("chan", "seq"),
    )
    return jax.shard_map(
        body, mesh=mesh, in_specs=placed, out_specs=P("chan", "seq"), check_vma=False
    )
```
